32 devices in a mesh: hid: 4 (over z), voc: 8 (over y, x, core).
Axes of the slice: x: 2, y: 2, z: 4, core: 2. Of those that a mesh axis runs over, the one named last changes fastest.
Arguments:
- hidden_states: bfloat16 [4096, 8192], P('voc', 'hid'), may hold values from -64 to 64
- positions: int32 [4, 64], replicated, may hold values from 0 to 1023, as said below
- norm_gain: float32 [8192], P('hid'), may hold values from 0.5 to 1.5
- embed_table: bfloat16 [31616, 8192], P('voc', 'hid'), may hold values from -5 to 5
Outputs:
- expected_embed: float32 [256, 8192], P('voc', 'hid')
- top_logprob: float32 [256], P('voc')
The draws below stay inside these ranges and needn't reach their ends.
Inputs may be any that keep to these rules, and one draw needn't show every extreme that they name: Within each request the 64 positions are distinct and include 0 and 1023.
All inputs are finite; a program needn't handle non-finite values.
Results may differ from the reference program's by a relative error of at most 0.015.
Values may be sent and summed in bfloat16 or wider, within the bound.
A program may use at most 64 MiB of HBM per device.

```python
import math
import jax
import jax.numpy as jnp
from jax import lax

D = 8192
REQUESTS = 4
MASKED = 64
SEQ = 1024
V = 31616


def table_rows(key, row_ids):
    table_key = jax.random.fold_in(key, 101)

    def one_row(row_id):
        return jnp.clip(jax.random.normal(jax.random.fold_in(table_key, row_id), (D,), jnp.float32), -5.0, 5.0)
    return jax.vmap(one_row)(row_ids)


def draw_embed_table(key, part):
    return table_rows(key, jnp.arange(V, dtype=jnp.int32)).astype(jnp.bfloat16)


def draw_norm_gain(key, part):
    return jax.random.uniform(jax.random.fold_in(key, 202), (D,), jnp.float32, 0.5, 1.5)


def pick_positions(key):
    pos_key = jax.random.fold_in(key, 303)

    def one_request(request):
        first_key, second_key = jax.random.split(jax.random.fold_in(pos_key, request))
        middle = jax.random.permutation(first_key, SEQ - 2)[:MASKED - 2].astype(jnp.int32) + 1
        every = jnp.concatenate([jnp.array([0, SEQ - 1], jnp.int32), middle])
        return every[jax.random.permutation(second_key, MASKED)].astype(jnp.int32)
    return jax.vmap(one_request)(jnp.arange(REQUESTS, dtype=jnp.int32))


def draw_positions(key, part):
    return pick_positions(key).astype(jnp.int32)


def draw_hidden_states(key, part):
    hid_key = jax.random.fold_in(key, 404)
    first_key = jax.random.fold_in(hid_key, 0)
    total_rows = REQUESTS * SEQ
    normal_rows = jax.random.normal(first_key, (total_rows, D), jnp.float32)
    ramp = jnp.linspace(1.0, 3.0, D)[None, :]
    result = jnp.clip(normal_rows * ramp, -16.0, 16.0)
    return result.astype(jnp.bfloat16)


def setup_inputs(seed: int = 0) -> dict:
    arg_keys = jax.random.split(jax.random.key(seed), 5)
    hidden_states = draw_hidden_states(jax.random.fold_in(arg_keys[4], 71), 0)
    positions = draw_positions(jax.random.fold_in(arg_keys[4], 71), 0)
    norm_gain = draw_norm_gain(jax.random.fold_in(arg_keys[4], 71), 0)
    embed_table = draw_embed_table(jax.random.fold_in(arg_keys[4], 71), 0)
    return dict(hidden_states=hidden_states, positions=positions, norm_gain=norm_gain, embed_table=embed_table)


norm_eps = 1e-05
logit_scale = 4.0

def reference(hidden_states, positions, norm_gain, embed_table):
    row_index = (jnp.arange(REQUESTS, dtype=jnp.int32)[:, None] * SEQ + positions).reshape(-1).astype(jnp.int32)
    picked = hidden_states[row_index].astype(jnp.float32)
    inverse = lax.rsqrt(lax.optimization_barrier(jnp.mean(picked * picked, axis=1)) + norm_eps) * (logit_scale / math.sqrt(D))
    scaled = (picked * norm_gain).astype(jnp.bfloat16)
    summed = lax.dot_general(scaled, embed_table, (((1,), (1,)), ((), ())), preferred_element_type=jnp.float32)
    logits = summed * inverse[:, None]
    row_max = lax.optimization_barrier(jnp.max(logits, axis=1))
    log_total = row_max + jnp.log(lax.optimization_barrier(jnp.sum(jnp.exp(logits - row_max[:, None]), axis=1)))
    probs = jnp.exp(logits - log_total[:, None]).astype(jnp.bfloat16)
    expected_embed = jnp.dot(probs, embed_table, preferred_element_type=jnp.float32)
    top_logprob = row_max - log_total
    return (expected_embed, top_logprob)
```

```python
import functools
import math

import jax
import jax.numpy as jnp
from jax import lax
from jax.experimental import pallas as pl
from jax.experimental.pallas import tpu as pltpu
from jax.sharding import PartitionSpec as P

norm_eps = 1e-05
logit_scale = 4.0
LINK = jnp.float32
TILE = 512
LANES = 128
SUB = 8
LOW = -1e30
MESH = pl.DeviceIdType.MESH


def as_row(column, lanes=LANES):
    return jnp.transpose(jnp.broadcast_to(column, (column.shape[0], lanes)))[:SUB]


def as_column(row):
    return jnp.transpose(jnp.broadcast_to(row, (LANES, row.shape[1])))[:, :1]


def kernel(
    sizes, hidden_hbm, pos_ref, gain_ref, table_hbm, out_ref, stat_ref,
    hid_v, table_v, part_out, picked_in, picked, scaled, square, sq_send, sq_recv,
    part, send_buf, recv_buf, run_max, run_sum, probs, stats, weights, acc, vx, v1, v2s, v2,
    load_sem, tab_sem, p1s, p1r, p2s, p2r, p3s, p3r, sqs, sqr, rss, rsr, ags, agr,
    sts, str_, ws, wr, e1s, e1r, e2s, e2r,
):
    n, nv, nr, width = sizes
    group = nv // nr
    h = lax.axis_index("hid")
    v = lax.axis_index("voc")
    r, g = v // group, lax.rem(v, group)
    local_rows, dl = hidden_hbm.shape
    vocab = table_hbm.shape[0]
    rows = pos_ref.shape[0]
    masked = rows // nr
    half = rows // 2
    tiles = part.shape[1]
    out_rows = rows // nv

    def remote(src, dst, ssem, rsem, **where):
        return pltpu.make_async_remote_copy(
            src_ref=src, dst_ref=dst, send_sem=ssem, recv_sem=rsem,
            device_id=where, device_id_type=MESH,
        )

    barrier = pltpu.get_barrier_semaphore()
    for k in range(1, n):
        pl.semaphore_signal(barrier, inc=1, device_id={"hid": lax.rem(h + k, n)}, device_id_type=MESH)
    for k in range(1, nv):
        pl.semaphore_signal(barrier, inc=1, device_id={"voc": lax.rem(v + k, nv)}, device_id_type=MESH)

    load = pltpu.make_async_copy(hidden_hbm, hid_v, load_sem)
    load.start()
    tab_copies = []
    for t in range(tiles):
        count = min(TILE, vocab - t * TILE)
        piece = pl.ds(t * TILE, count)
        tab_copies.append(pltpu.make_async_copy(table_hbm.at[piece], table_v.at[piece], tab_sem.at[t]))
        tab_copies[-1].start()
    if tiles * TILE > vocab:
        table_v[pl.ds(vocab, tiles * TILE - vocab), :] = jnp.zeros(
            (tiles * TILE - vocab, dl), table_v.dtype
        )

    load.wait()
    want = pos_ref[pl.ds(pl.multiple_of(r * masked, masked), masked), :]
    have = lax.broadcasted_iota(jnp.int32, (masked, local_rows), 1) + g * local_rows
    one_hot = jnp.where(want == have, 1.0, 0.0).astype(jnp.bfloat16)
    mine = jnp.dot(one_hot, hid_v[...], preferred_element_type=jnp.float32)
    part_out[...] = mine.reshape(group, masked // group, dl).astype(jnp.bfloat16)

    pl.semaphore_wait(barrier, n - 1 + nv - 1)

    for k in range(1, group):
        to = lax.rem(g + k, group)
        remote(part_out.at[to], picked_in.at[g], p1s.at[to], p1r.at[g], voc=r * group + to).start()
    total = part_out[g].astype(jnp.float32)
    for k in range(1, group):
        src = lax.rem(g + k, group)
        remote(part_out.at[src], picked_in.at[src], p1s.at[src], p1r.at[src], voc=r * group + src).wait_recv()
        total += picked_in[src].astype(jnp.float32)
    picked[v] = total.astype(jnp.bfloat16)
    for k in range(1, nr):
        to = lax.rem(r + k, nr)
        remote(picked.at[v], picked.at[v], p2s.at[to], p2r.at[r], voc=to * group + g).start()
    for k in range(nr):
        src = lax.rem(r + k, nr)
        slot = src * group + g
        if k:
            remote(picked.at[slot], picked.at[slot], p2s.at[src], p2r.at[src], voc=slot).wait_recv()
        for j in range(1, group):
            to = lax.rem(g + j, group)
            remote(
                picked.at[slot], picked.at[slot], p3s.at[src, to], p3r.at[src, g], voc=r * group + to
            ).start()
    for k in range(nr):
        src = lax.rem(r + k, nr)
        for j in range(1, group):
            seat = lax.rem(g + j, group)
            slot = src * group + seat
            remote(
                picked.at[slot], picked.at[slot], p3s.at[src, seat], p3r.at[src, seat], voc=r * group + seat
            ).wait_recv()
    gain = gain_ref[...]
    for k in range(nr):
        x = picked[k * group : (k + 1) * group].astype(jnp.float32).reshape(masked, dl)
        square[k * masked : (k + 1) * masked, :] = jnp.broadcast_to(
            jnp.sum(x * x, axis=1, keepdims=True), (masked, LANES)
        )
        scaled[k * masked : (k + 1) * masked, :] = (x * gain).astype(jnp.bfloat16)

    places = (h, n - 1 - h)
    ends = (n - 1, 0)
    steps = (1, -1)
    for side in range(2):
        sq_send[side] = jnp.transpose(square[side * half : (side + 1) * half, :])[:SUB]

        @pl.when(places[side] < n - 1)
        def _(side=side):
            remote(sq_send.at[side], sq_recv.at[h], sqs.at[side], sqr.at[h], hid=ends[side]).start()

    for copy in tab_copies:
        copy.wait()
    run_max[...] = jnp.full(run_max.shape, LOW, jnp.float32)
    run_sum[...] = jnp.zeros_like(run_sum)
    acc[...] = jnp.zeros_like(acc)
    limit = vocab - (tiles - 1) * TILE

    def chain(side, t):
        src = part.at[side, t] if send_buf is None else send_buf.at[side, t]
        to = jnp.clip(h + steps[side], 0, n - 1)
        return remote(src, recv_buf.at[side, t], rss.at[side, t], rsr.at[side, t], hid=to)

    def sum_step(s, carry):
        @pl.when(s < tiles)
        def _():
            piece = pl.ds(pl.multiple_of(s * TILE, TILE), TILE)
            both = lax.dot_general(
                scaled[...], table_v[piece, :], (((1,), (1,)), ((), ())),
                preferred_element_type=jnp.float32,
            )
            part[0, s] = both[:half]
            part[1, s] = both[half:]

        for side in range(2):
            place = places[side]
            t = s - place

            @pl.when((t >= 0) & (t < tiles))
            def _(side=side, place=place, t=t):
                @pl.when(place > 0)
                def _():
                    chain(side, t).wait_recv()
                    part[side, t] += recv_buf[side, t].astype(jnp.float32)

                @pl.when(place < n - 1)
                def _():
                    if send_buf is not None:
                        send_buf[side, t] = part[side, t].astype(LINK)
                    chain(side, t).start()

                @pl.when(place == n - 1)
                def _():
                    @pl.when(t == tiles - 1)
                    def _():
                        column = lax.broadcasted_iota(jnp.int32, (half, TILE), 1)
                        part[side, t] = jnp.where(column < limit, part[side, t], LOW)

                    top = run_max[...]
                    for c in range(0, TILE, LANES):
                        top = jnp.maximum(top, part[side, t, :, c : c + LANES])
                    run_max[...] = top

        return carry

    lax.fori_loop(0, tiles + n - 1, sum_step, 0)

    def spread(side, t):
        to = jnp.clip(h - steps[side], 0, n - 1)
        return remote(probs.at[side, t], probs.at[side, t], ags.at[side, t], agr.at[side, t], hid=to)

    for side in range(2):

        @pl.when(places[side] == n - 1)
        def _(side=side):
            squares = sq_send[side]
            for k in range(1, n):
                src = lax.rem(h + k, n)
                remote(sq_send.at[side], sq_recv.at[src], sqs.at[side], sqr.at[src], hid=src).wait_recv()
                squares += sq_recv[src]
            inverse = as_column(
                lax.rsqrt(squares[:1] / width + norm_eps) * (logit_scale / math.sqrt(width))
            )
            top = jnp.max(run_max[...], axis=1, keepdims=True) * inverse

            def exp_step(t, carry):
                e = jnp.exp(part[side, t] * inverse - top)
                probs[side, t] = e.astype(jnp.bfloat16)
                spread(side, t).start()
                more = run_sum[...]
                for c in range(0, TILE, LANES):
                    more += e[:, c : c + LANES]
                run_sum[...] = more
                return carry

            lax.fori_loop(0, tiles, exp_step, 0)
            stats[v, 0] = as_row(top)
            stats[v, 1] = as_row(jnp.sum(run_sum[...], axis=1, keepdims=True))
            for k in range(1, nv):
                to = lax.rem(v + k, nv)
                remote(stats.at[v], stats.at[v], sts.at[to], str_.at[v], voc=to).start()
            for k in range(1, nv):
                src = lax.rem(v + k, nv)
                remote(stats.at[src], stats.at[src], sts.at[src], str_.at[src], voc=src).wait_recv()
            high = stats[0, 0]
            for k in range(1, nv):
                high = jnp.maximum(high, stats[k, 0])
            total = jnp.zeros_like(high)
            for k in range(nv):
                total += stats[k, 1] * jnp.exp(stats[k, 0] - high)
            weights[side, 0] = jnp.exp(stats[v, 0] - high) / total
            weights[side, 1] = high - (high + jnp.log(total))
            for k in range(1, n):
                to = lax.rem(h + k, n)
                remote(weights.at[side], weights.at[side], ws.at[to], wr.at[side], hid=to).start()

    lag = jnp.maximum(h, n - 1 - h)

    def mix_step(s, carry):
        for side in range(2):
            place = places[side]
            t = s - (n - 1 - place)

            @pl.when((t >= 0) & (t < tiles) & (place < n - 1))
            def _(side=side, place=place, t=t):
                spread(side, t).wait_recv()

                @pl.when(place > 0)
                def _():
                    spread(side, t).start()

        m = s - lag

        @pl.when((m >= 0) & (m < tiles))
        def _():
            piece = pl.ds(pl.multiple_of(m * TILE, TILE), TILE)
            both = jnp.concatenate([probs[0, m], probs[1, m]], axis=0)
            step = min(dl, 512)
            for c in range(0, dl, step):
                acc[:, c : c + step] += jnp.dot(
                    both, table_v[piece, c : c + step], preferred_element_type=jnp.float32
                )

        return carry

    lax.fori_loop(0, tiles + n - 1, mix_step, 0)

    for side in range(2):

        @pl.when(places[side] < n - 1)
        def _(side=side):
            remote(
                weights.at[side], weights.at[side], ws.at[ends[side]], wr.at[side], hid=ends[side]
            ).wait_recv()

        scale = as_column(weights[side, 0, :1])
        span = slice(side * half, (side + 1) * half)
        acc[span, :] = acc[span, :] * scale
    stat_ref[...] = weights[...]

    def block(seat, k):
        start = pl.multiple_of((k * group + seat) * out_rows, out_rows)
        return acc[pl.ds(start, out_rows), :]

    for k in range(nr):
        there = lax.rem(r + k + 1, nr)
        for j in range(1, group):
            to = lax.rem(g + j, group)
            vx[to, there] = block(to, there).astype(jnp.bfloat16)
            remote(
                vx.at[to, there], v1.at[g, there], e1s.at[to, there], e1r.at[g, there], voc=r * group + to
            ).start()
    total = None
    for k in range(nr):
        there = lax.rem(r + k + 1, nr)
        total = block(g, there)
        for j in range(1, group):
            src = lax.rem(g + j, group)
            remote(
                vx.at[src, there], v1.at[src, there], e1s.at[src, there], e1r.at[src, there],
                voc=r * group + src,
            ).wait_recv()
            total += v1[src, there].astype(jnp.float32)
        if k < nr - 1:
            v2s[there] = total.astype(jnp.bfloat16)
            remote(v2s.at[there], v2.at[r], e2s.at[there], e2r.at[r], voc=there * group + g).start()
        else:
            out_ref[...] = total
    for k in range(1, nr):
        src = lax.rem(r + k, nr)
        remote(v2s.at[src], v2.at[src], e2s.at[src], e2r.at[src], voc=src * group + g).wait_recv()
        out_ref[...] += v2[src].astype(jnp.float32)

    for k in range(1, group):
        to = lax.rem(g + k, group)
        remote(part_out.at[to], picked_in.at[g], p1s.at[to], p1r.at[g], voc=r * group + to).wait_send()
    for k in range(nr):
        src = lax.rem(r + k, nr)
        slot = src * group + g
        if k:
            remote(picked.at[v], picked.at[v], p2s.at[src], p2r.at[r], voc=slot).wait_send()
            remote(v2s.at[src], v2.at[r], e2s.at[src], e2r.at[r], voc=slot).wait_send()
        for j in range(1, group):
            to = lax.rem(g + j, group)
            mate = r * group + to
            remote(picked.at[slot], picked.at[slot], p3s.at[src, to], p3r.at[src, g], voc=mate).wait_send()
            remote(vx.at[to, src], v1.at[g, src], e1s.at[to, src], e1r.at[g, src], voc=mate).wait_send()
    for side in range(2):

        @pl.when(places[side] < n - 1)
        def _(side=side):
            remote(sq_send.at[side], sq_recv.at[h], sqs.at[side], sqr.at[h], hid=ends[side]).wait_send()

        @pl.when(places[side] == n - 1)
        def _(side=side):
            for k in range(1, nv):
                to = lax.rem(v + k, nv)
                remote(stats.at[v], stats.at[v], sts.at[to], str_.at[v], voc=to).wait_send()
            for k in range(1, n):
                to = lax.rem(h + k, n)
                remote(weights.at[side], weights.at[side], ws.at[to], wr.at[side], hid=to).wait_send()

        def drain(t, carry, side=side):
            @pl.when(places[side] < n - 1)
            def _():
                chain(side, t).wait_send()

            @pl.when(places[side] > 0)
            def _():
                spread(side, t).wait_send()

            return carry

        lax.fori_loop(0, tiles, drain, 0)


def local(width, hidden_states, positions, norm_gain, embed_table):
    nr, masked = positions.shape
    rows = nr * masked
    n, nv = lax.axis_size("hid"), lax.axis_size("voc")
    group = nv // nr
    local_rows, dl = hidden_states.shape
    vocab = embed_table.shape[0]
    tiles = pl.cdiv(vocab, TILE)
    half, out_rows = rows // 2, rows // nv
    bf16, f32 = jnp.bfloat16, jnp.float32
    narrow = LINK != jnp.float32
    dma = pltpu.SemaphoreType.DMA
    vmem = pl.BlockSpec(memory_space=pltpu.VMEM)
    hbm = pl.BlockSpec(memory_space=pl.ANY)
    scratch = [
        pltpu.VMEM((local_rows, dl), bf16),
        pltpu.VMEM((tiles * TILE, dl), bf16),
        pltpu.VMEM((group, masked // group, dl), bf16),
        pltpu.VMEM((group, masked // group, dl), bf16),
        pltpu.VMEM((nv, masked // group, dl), bf16),
        pltpu.VMEM((rows, dl), bf16),
        pltpu.VMEM((rows, LANES), f32),
        pltpu.VMEM((2, SUB, half), f32),
        pltpu.VMEM((n, SUB, half), f32),
        pltpu.VMEM((2, tiles, half, TILE), f32),
        pltpu.VMEM((2, tiles, half, TILE), LINK) if narrow else None,
        pltpu.VMEM((2, tiles, half, TILE), LINK),
        pltpu.VMEM((half, LANES), f32),
        pltpu.VMEM((half, LANES), f32),
        pltpu.VMEM((2, tiles, half, TILE), bf16),
        pltpu.VMEM((nv, 2, SUB, half), f32),
        pltpu.VMEM((2, 2, SUB, half), f32),
        pltpu.VMEM((rows, dl), f32),
        pltpu.VMEM((group, nr, out_rows, dl), bf16),
        pltpu.VMEM((group, nr, out_rows, dl), bf16),
        pltpu.VMEM((nr, out_rows, dl), bf16),
        pltpu.VMEM((nr, out_rows, dl), bf16),
        dma, dma((tiles,)),
        dma((group,)), dma((group,)), dma((nr,)), dma((nr,)), dma((nr, group)), dma((nr, group)),
        dma((2,)), dma((n,)),
        dma((2, tiles)), dma((2, tiles)), dma((2, tiles)), dma((2, tiles)),
        dma((nv,)), dma((nv,)), dma((n,)), dma((2,)),
        dma((group, nr)), dma((group, nr)), dma((nr,)), dma((nr,)),
    ]
    absent = 6 + 10
    body = functools.partial(kernel, (n, nv, nr, width))
    if not narrow:
        scratch = [s for s in scratch if s is not None]

        def body(*refs):
            kernel((n, nv, nr, width), *refs[:absent], None, *refs[absent:])

    expected, stat = pl.pallas_call(
        body,
        out_shape=(
            jax.ShapeDtypeStruct((out_rows, dl), f32),
            jax.ShapeDtypeStruct((2, 2, SUB, half), f32),
        ),
        in_specs=[hbm, vmem, vmem, hbm],
        out_specs=(vmem, vmem),
        scratch_shapes=scratch,
        compiler_params=pltpu.CompilerParams(
            collective_id=0, has_side_effects=True, vmem_limit_bytes=60 * 1024 * 1024
        ),
        name="head",
    )(hidden_states, positions.reshape(rows, 1), norm_gain.reshape(1, dl), embed_table)
    top = lax.dynamic_slice_in_dim(
        stat[:, 1, 0, :].reshape(rows), lax.axis_index("voc") * out_rows, out_rows, 0
    )
    return expected, top


def solution(mesh):
    def whole(hidden_states, positions, norm_gain, embed_table):
        return jax.shard_map(
            functools.partial(local, hidden_states.shape[1]),
            mesh=mesh,
            in_specs=(P("voc", "hid"), P(), P("hid"), P("voc", "hid")),
            out_specs=(P("voc", "hid"), P("voc")),
            check_vma=False,
        )(hidden_states, positions, norm_gain, embed_table)

    return whole
```

```python
import functools
import math

import jax
import jax.numpy as jnp
from jax import lax
from jax.experimental import pallas as pl
from jax.experimental.pallas import tpu as pltpu
from jax.sharding import PartitionSpec as P

norm_eps = 1e-05
logit_scale = 4.0
LINK = jnp.float32
TILE = 128
PAIR = 2
GAP = 4
BATCH = 512
LANES = 128
SUB = 8
LOW = -1e30
MESH = pl.DeviceIdType.MESH


def as_row(column, lanes=LANES):
    return jnp.transpose(jnp.broadcast_to(column, (column.shape[0], lanes)))[:SUB]


def as_column(row):
    return jnp.transpose(jnp.broadcast_to(row, (LANES, row.shape[1])))[:, :1]


def kernel(
    sizes, hidden_hbm, pos_ref, gain_ref, table_hbm, out_ref, stat_ref,
    hid_v, table_v, part_out, picked_in, picked, scaled, square, sq_send, sq_recv,
    part, send_buf, recv_buf, run_max, run_sum, probs, stats, weights, acc, vx, v1, v2s, v2,
    load_sem, tab_sem, p1s, p1r, p2s, p2r, p3s, p3r, sqs, sqr, rss, rsr, ags, agr,
    sts, str_, ws, wr, e1s, e1r, e2s, e2r,
):
    n, nv, nr, width = sizes
    group = nv // nr
    h = lax.axis_index("hid")
    v = lax.axis_index("voc")
    r, g = v // group, lax.rem(v, group)
    local_rows, dl = hidden_hbm.shape
    vocab = table_hbm.shape[0]
    masked = pos_ref.shape[1]
    rows = nr * masked
    half = rows // 2
    tiles = -(-vocab // TILE)
    slots = part.shape[1]
    out_rows = rows // nv

    def remote(src, dst, ssem, rsem, **where):
        return pltpu.make_async_remote_copy(
            src_ref=src, dst_ref=dst, send_sem=ssem, recv_sem=rsem,
            device_id=where, device_id_type=MESH,
        )

    barrier = pltpu.get_barrier_semaphore()
    for k in range(1, n):
        pl.semaphore_signal(barrier, inc=1, device_id={"hid": lax.rem(h + k, n)}, device_id_type=MESH)
    for k in range(1, nv):
        pl.semaphore_signal(barrier, inc=1, device_id={"voc": lax.rem(v + k, nv)}, device_id_type=MESH)

    load = pltpu.make_async_copy(hidden_hbm, hid_v, load_sem)
    load.start()
    padded = table_v.shape[0]
    if padded > vocab:
        table_v[pl.ds(vocab, padded - vocab), :] = jnp.zeros((padded - vocab, dl), table_v.dtype)

    want = as_column(pos_ref[pl.ds(r, 1), :].astype(jnp.float32))
    have = (lax.broadcasted_iota(jnp.int32, (masked, local_rows), 1) + g * local_rows).astype(jnp.float32)
    load.wait()
    tab_copies = []
    for first in range(0, vocab, BATCH):
        piece = pl.ds(first, min(BATCH, vocab - first))
        tab_copies.append(
            pltpu.make_async_copy(table_hbm.at[piece], table_v.at[piece], tab_sem.at[first // BATCH])
        )
        tab_copies[-1].start()
    one_hot = jnp.where(want == have, 1.0, 0.0).astype(jnp.bfloat16)
    mine = jnp.dot(one_hot, hid_v[...], preferred_element_type=jnp.float32)
    part_out[...] = mine.reshape(group, masked // group, dl).astype(jnp.bfloat16)

    pl.semaphore_wait(barrier, n - 1 + nv - 1)

    for k in range(1, group):
        to = lax.rem(g + k, group)
        remote(part_out.at[to], picked_in.at[g], p1s.at[to], p1r.at[g], voc=r * group + to).start()
    total = part_out[g].astype(jnp.float32)
    for k in range(1, group):
        src = lax.rem(g + k, group)
        remote(part_out.at[src], picked_in.at[src], p1s.at[src], p1r.at[src], voc=r * group + src).wait_recv()
        total += picked_in[src].astype(jnp.float32)
    picked[v] = total.astype(jnp.bfloat16)
    for k in range(1, nr):
        to = lax.rem(r + k, nr)
        remote(picked.at[v], picked.at[v], p2s.at[to], p2r.at[r], voc=to * group + g).start()
    for k in range(nr):
        src = lax.rem(r + k, nr)
        slot = src * group + g
        if k:
            remote(picked.at[slot], picked.at[slot], p2s.at[src], p2r.at[src], voc=slot).wait_recv()
        for j in range(1, group):
            to = lax.rem(g + j, group)
            remote(
                picked.at[slot], picked.at[slot], p3s.at[src, to], p3r.at[src, g], voc=r * group + to
            ).start()
    for k in range(nr):
        src = lax.rem(r + k, nr)
        for j in range(1, group):
            seat = lax.rem(g + j, group)
            slot = src * group + seat
            remote(
                picked.at[slot], picked.at[slot], p3s.at[src, seat], p3r.at[src, seat], voc=r * group + seat
            ).wait_recv()
    gain = gain_ref[...]
    for k in range(nr):
        x = picked[k * group : (k + 1) * group].astype(jnp.float32).reshape(masked, dl)
        square[k * masked : (k + 1) * masked, :] = jnp.broadcast_to(
            jnp.sum(x * x, axis=1, keepdims=True), (masked, LANES)
        )
        scaled[k * masked : (k + 1) * masked, :] = (x * gain).astype(jnp.bfloat16)

    places = (h, n - 1 - h)
    ends = (n - 1, 0)
    steps = (1, -1)
    for side in range(2):
        sq_send[side] = jnp.transpose(square[side * half : (side + 1) * half, :])[:SUB]

        @pl.when(places[side] < n - 1)
        def _(side=side):
            remote(sq_send.at[side], sq_recv.at[h], sqs.at[side], sqr.at[h], hid=ends[side]).start()

    for copy in tab_copies:
        copy.wait()
    run_max[...] = jnp.full(run_max.shape, LOW, jnp.float32)
    run_sum[...] = jnp.zeros_like(run_sum)
    acc[...] = jnp.zeros_like(acc)
    limit = vocab - (tiles - 1) * TILE

    def chain(side, t):
        src = part.at[side, t] if send_buf is None else send_buf.at[side, t]
        to = jnp.clip(h + steps[side], 0, n - 1)
        return remote(src, recv_buf.at[side, t], rss.at[side, t], rsr.at[side, t], hid=to)

    def sum_step(s, carry):
        @pl.when((s < slots) & (lax.rem(s, PAIR) == 0))
        def _():
            piece = pl.ds(pl.multiple_of(s * TILE, TILE), PAIR * TILE)
            both = lax.dot_general(
                scaled[...], table_v[piece, :], (((1,), (1,)), ((), ())),
                preferred_element_type=jnp.float32,
            )
            for k in range(PAIR):
                part[0, s + k] = both[:half, k * TILE : (k + 1) * TILE]
                part[1, s + k] = both[half:, k * TILE : (k + 1) * TILE]

        for side in range(2):
            place = places[side]
            t = s - GAP * place

            @pl.when((t >= 0) & (t < tiles))
            def _(side=side, place=place, t=t):
                @pl.when(place > 0)
                def _():
                    chain(side, t).wait_recv()
                    part[side, t] += recv_buf[side, t].astype(jnp.float32)

                @pl.when(place < n - 1)
                def _():
                    if send_buf is not None:
                        send_buf[side, t] = part[side, t].astype(LINK)
                    chain(side, t).start()

                @pl.when(place == n - 1)
                def _():
                    @pl.when(t == tiles - 1)
                    def _():
                        column = lax.broadcasted_iota(jnp.int32, (half, TILE), 1)
                        part[side, t] = jnp.where(column < limit, part[side, t], LOW)

                    top = run_max[...]
                    for c in range(0, TILE, LANES):
                        top = jnp.maximum(top, part[side, t, :, c : c + LANES])
                    run_max[...] = top

        return carry

    lax.fori_loop(0, tiles + GAP * (n - 1), sum_step, 0)

    def spread(side, t):
        to = jnp.clip(h - steps[side], 0, n - 1)
        return remote(probs.at[side, t], probs.at[side, t], ags.at[side, t], agr.at[side, t], hid=to)

    for side in range(2):

        @pl.when(places[side] == n - 1)
        def _(side=side):
            squares = sq_send[side]
            for k in range(1, n):
                src = lax.rem(h + k, n)
                remote(sq_send.at[side], sq_recv.at[src], sqs.at[side], sqr.at[src], hid=src).wait_recv()
                squares += sq_recv[src]
            inverse = as_column(
                lax.rsqrt(squares[:1] / width + norm_eps) * (logit_scale / math.sqrt(width))
            )
            top = jnp.max(run_max[...], axis=1, keepdims=True) * inverse

            def exp_step(t, carry):
                e = jnp.exp(part[side, t] * inverse - top)
                probs[side, t] = e.astype(jnp.bfloat16)
                spread(side, t).start()
                more = run_sum[...]
                for c in range(0, TILE, LANES):
                    more += e[:, c : c + LANES]
                run_sum[...] = more
                return carry

            lax.fori_loop(0, tiles, exp_step, 0)
            stats[v, 0] = as_row(top)
            stats[v, 1] = as_row(jnp.sum(run_sum[...], axis=1, keepdims=True))
            for k in range(1, nv):
                to = lax.rem(v + k, nv)
                remote(stats.at[v], stats.at[v], sts.at[to], str_.at[v], voc=to).start()
            for k in range(1, nv):
                src = lax.rem(v + k, nv)
                remote(stats.at[src], stats.at[src], sts.at[src], str_.at[src], voc=src).wait_recv()
            high = stats[0, 0]
            for k in range(1, nv):
                high = jnp.maximum(high, stats[k, 0])
            total = jnp.zeros_like(high)
            for k in range(nv):
                total += stats[k, 1] * jnp.exp(stats[k, 0] - high)
            weights[side, 0] = jnp.exp(stats[v, 0] - high) / total
            weights[side, 1] = high - (high + jnp.log(total))
            for k in range(1, n):
                to = lax.rem(h + k, n)
                remote(weights.at[side], weights.at[side], ws.at[to], wr.at[side], hid=to).start()

    for t in range(tiles, slots):
        probs[:, t] = jnp.zeros((2, half, TILE), probs.dtype)
    lag = GAP * jnp.maximum(h, n - 1 - h)

    def mix_step(s, carry):
        for side in range(2):
            place = places[side]
            t = s - GAP * (n - 1 - place)

            @pl.when((t >= 0) & (t < tiles) & (place < n - 1))
            def _(side=side, place=place, t=t):
                spread(side, t).wait_recv()

                @pl.when(place > 0)
                def _():
                    spread(side, t).start()

        m = s - lag

        @pl.when((m >= 0) & (m < slots) & (lax.rem(m, PAIR) == PAIR - 1))
        def _():
            first = m - (PAIR - 1)
            piece = pl.ds(pl.multiple_of(first * TILE, PAIR * TILE), PAIR * TILE)
            both = jnp.concatenate(
                [
                    jnp.concatenate([probs[side, first + k] for k in range(PAIR)], axis=1)
                    for side in range(2)
                ],
                axis=0,
            )
            step = min(dl, 512)
            for c in range(0, dl, step):
                acc[:, c : c + step] += jnp.dot(
                    both, table_v[piece, c : c + step], preferred_element_type=jnp.float32
                )

        return carry

    lax.fori_loop(0, slots + GAP * (n - 1), mix_step, 0)

    for side in range(2):

        @pl.when(places[side] < n - 1)
        def _(side=side):
            remote(
                weights.at[side], weights.at[side], ws.at[ends[side]], wr.at[side], hid=ends[side]
            ).wait_recv()

        scale = as_column(weights[side, 0, :1])
        span = slice(side * half, (side + 1) * half)
        acc[span, :] = acc[span, :] * scale
    first = v * out_rows
    log_top = as_column(weights[first // half, 1, :1])
    row_of = lax.broadcasted_iota(jnp.int32, (half, out_rows), 0)
    place_of = lax.broadcasted_iota(jnp.int32, (half, out_rows), 1) + lax.rem(first, half)
    stat_ref[...] = jnp.sum(jnp.where(row_of == place_of, log_top, 0.0), axis=0, keepdims=True)

    def block(seat, k):
        start = pl.multiple_of((k * group + seat) * out_rows, out_rows)
        return acc[pl.ds(start, out_rows), :]

    for k in range(nr):
        there = lax.rem(r + k + 1, nr)
        for j in range(1, group):
            to = lax.rem(g + j, group)
            vx[to, there] = block(to, there).astype(jnp.bfloat16)
            remote(
                vx.at[to, there], v1.at[g, there], e1s.at[to, there], e1r.at[g, there], voc=r * group + to
            ).start()
    total = None
    for k in range(nr):
        there = lax.rem(r + k + 1, nr)
        total = block(g, there)
        for j in range(1, group):
            src = lax.rem(g + j, group)
            remote(
                vx.at[src, there], v1.at[src, there], e1s.at[src, there], e1r.at[src, there],
                voc=r * group + src,
            ).wait_recv()
            total += v1[src, there].astype(jnp.float32)
        if k < nr - 1:
            v2s[there] = total.astype(jnp.bfloat16)
            remote(v2s.at[there], v2.at[r], e2s.at[there], e2r.at[r], voc=there * group + g).start()
        else:
            out_ref[...] = total
    for k in range(1, nr):
        src = lax.rem(r + k, nr)
        remote(v2s.at[src], v2.at[src], e2s.at[src], e2r.at[src], voc=src * group + g).wait_recv()
        out_ref[...] += v2[src].astype(jnp.float32)

    for k in range(1, group):
        to = lax.rem(g + k, group)
        remote(part_out.at[to], picked_in.at[g], p1s.at[to], p1r.at[g], voc=r * group + to).wait_send()
    for k in range(nr):
        src = lax.rem(r + k, nr)
        slot = src * group + g
        if k:
            remote(picked.at[v], picked.at[v], p2s.at[src], p2r.at[r], voc=slot).wait_send()
            remote(v2s.at[src], v2.at[r], e2s.at[src], e2r.at[r], voc=slot).wait_send()
        for j in range(1, group):
            to = lax.rem(g + j, group)
            mate = r * group + to
            remote(picked.at[slot], picked.at[slot], p3s.at[src, to], p3r.at[src, g], voc=mate).wait_send()
            remote(vx.at[to, src], v1.at[g, src], e1s.at[to, src], e1r.at[g, src], voc=mate).wait_send()
    for side in range(2):

        @pl.when(places[side] < n - 1)
        def _(side=side):
            remote(sq_send.at[side], sq_recv.at[h], sqs.at[side], sqr.at[h], hid=ends[side]).wait_send()

        @pl.when(places[side] == n - 1)
        def _(side=side):
            for k in range(1, nv):
                to = lax.rem(v + k, nv)
                remote(stats.at[v], stats.at[v], sts.at[to], str_.at[v], voc=to).wait_send()
            for k in range(1, n):
                to = lax.rem(h + k, n)
                remote(weights.at[side], weights.at[side], ws.at[to], wr.at[side], hid=to).wait_send()

        def drain(t, carry, side=side):
            @pl.when(places[side] < n - 1)
            def _():
                chain(side, t).wait_send()

            @pl.when(places[side] > 0)
            def _():
                spread(side, t).wait_send()

            return carry

        lax.fori_loop(0, tiles, drain, 0)


def local(width, hidden_states, positions, norm_gain, embed_table):
    nr, masked = positions.shape
    rows = nr * masked
    n, nv = lax.axis_size("hid"), lax.axis_size("voc")
    group = nv // nr
    local_rows, dl = hidden_states.shape
    vocab = embed_table.shape[0]
    tiles = pl.cdiv(vocab, TILE)
    slots = pl.cdiv(tiles, PAIR) * PAIR
    half, out_rows = rows // 2, rows // nv
    bf16, f32 = jnp.bfloat16, jnp.float32
    narrow = LINK != jnp.float32
    dma = pltpu.SemaphoreType.DMA
    vmem = pl.BlockSpec(memory_space=pltpu.VMEM)
    hbm = pl.BlockSpec(memory_space=pl.ANY)
    scratch = [
        pltpu.VMEM((local_rows, dl), bf16),
        pltpu.VMEM((slots * TILE, dl), bf16),
        pltpu.VMEM((group, masked // group, dl), bf16),
        pltpu.VMEM((group, masked // group, dl), bf16),
        pltpu.VMEM((nv, masked // group, dl), bf16),
        pltpu.VMEM((rows, dl), bf16),
        pltpu.VMEM((rows, LANES), f32),
        pltpu.VMEM((2, SUB, half), f32),
        pltpu.VMEM((n, SUB, half), f32),
        pltpu.VMEM((2, slots, half, TILE), f32),
        pltpu.VMEM((2, tiles, half, TILE), LINK) if narrow else None,
        pltpu.VMEM((2, tiles, half, TILE), LINK),
        pltpu.VMEM((half, LANES), f32),
        pltpu.VMEM((half, LANES), f32),
        pltpu.VMEM((2, slots, half, TILE), bf16),
        pltpu.VMEM((nv, 2, SUB, half), f32),
        pltpu.VMEM((2, 2, SUB, half), f32),
        pltpu.VMEM((rows, dl), f32),
        pltpu.VMEM((group, nr, out_rows, dl), bf16),
        pltpu.VMEM((group, nr, out_rows, dl), bf16),
        pltpu.VMEM((nr, out_rows, dl), bf16),
        pltpu.VMEM((nr, out_rows, dl), bf16),
        dma, dma((pl.cdiv(vocab, BATCH),)),
        dma((group,)), dma((group,)), dma((nr,)), dma((nr,)), dma((nr, group)), dma((nr, group)),
        dma((2,)), dma((n,)),
        dma((2, tiles)), dma((2, tiles)), dma((2, tiles)), dma((2, tiles)),
        dma((nv,)), dma((nv,)), dma((n,)), dma((2,)),
        dma((group, nr)), dma((group, nr)), dma((nr,)), dma((nr,)),
    ]
    absent = 6 + 10
    body = functools.partial(kernel, (n, nv, nr, width))
    if not narrow:
        scratch = [s for s in scratch if s is not None]

        def body(*refs):
            kernel((n, nv, nr, width), *refs[:absent], None, *refs[absent:])

    expected, stat = pl.pallas_call(
        body,
        out_shape=(
            jax.ShapeDtypeStruct((out_rows, dl), f32),
            jax.ShapeDtypeStruct((1, out_rows), f32),
        ),
        in_specs=[hbm, vmem, vmem, hbm],
        out_specs=(vmem, vmem),
        scratch_shapes=scratch,
        compiler_params=pltpu.CompilerParams(
            collective_id=0, has_side_effects=True, vmem_limit_bytes=60 * 1024 * 1024
        ),
        name="head",
    )(hidden_states, positions, norm_gain.reshape(1, dl), embed_table)
    return expected, stat.reshape(out_rows)


def solution(mesh):
    def whole(hidden_states, positions, norm_gain, embed_table):
        return jax.shard_map(
            functools.partial(local, hidden_states.shape[1]),
            mesh=mesh,
            in_specs=(P("voc", "hid"), P(), P("hid"), P("voc", "hid")),
            out_specs=(P("voc", "hid"), P("voc")),
            check_vma=False,
        )(hidden_states, positions, norm_gain, embed_table)

    return whole
```

```python
import functools
import math

import jax
import jax.numpy as jnp
from jax import lax
from jax.experimental import pallas as pl
from jax.experimental.pallas import tpu as pltpu
from jax.sharding import PartitionSpec as P

norm_eps = 1e-05
logit_scale = 4.0
LINK = jnp.float32
TILE = 128
PAIR = 2
GAP = 4
BATCH = 512
LANES = 128
SUB = 8
LOW = -1e30
MESH = pl.DeviceIdType.MESH


def as_row(column, lanes=LANES):
    return jnp.transpose(jnp.broadcast_to(column, (column.shape[0], lanes)))[:SUB]


def as_column(row):
    return jnp.transpose(jnp.broadcast_to(row, (LANES, row.shape[1])))[:, :1]


def kernel(
    sizes, hidden_hbm, pos_ref, gain_ref, table_hbm, out_ref, stat_ref,
    hid_v, table_v, part_out, picked_in, picked, scaled, square, sq_send, sq_recv,
    part, send_buf, recv_buf, run_max, run_sum, probs, stats, weights, acc, vx, v1, v2s, v2,
    load_sem, tab_sem, p1s, p1r, p2s, p2r, p3s, p3r, sqs, sqr, rss, rsr, ags, agr,
    sts, str_, ws, wr, e1s, e1r, e2s, e2r,
):
    n, nv, nr, width = sizes
    group = nv // nr
    h = lax.axis_index("hid")
    v = lax.axis_index("voc")
    r, g = v // group, lax.rem(v, group)
    local_rows, dl = hidden_hbm.shape
    vocab = table_hbm.shape[0]
    masked = pos_ref.shape[1]
    rows = nr * masked
    half = rows // 2
    tiles = -(-vocab // TILE)
    slots = part.shape[1]
    out_rows = rows // nv

    def remote(src, dst, ssem, rsem, **where):
        return pltpu.make_async_remote_copy(
            src_ref=src, dst_ref=dst, send_sem=ssem, recv_sem=rsem,
            device_id=where, device_id_type=MESH,
        )

    barrier = pltpu.get_barrier_semaphore()
    for k in range(1, n):
        pl.semaphore_signal(barrier, inc=1, device_id={"hid": lax.rem(h + k, n)}, device_id_type=MESH)
    for k in range(1, nv):
        pl.semaphore_signal(barrier, inc=1, device_id={"voc": lax.rem(v + k, nv)}, device_id_type=MESH)

    load = pltpu.make_async_copy(hidden_hbm, hid_v, load_sem)
    load.start()
    padded = table_v.shape[0]
    if padded > vocab:
        table_v[pl.ds(vocab, padded - vocab), :] = jnp.zeros((padded - vocab, dl), table_v.dtype)

    want = as_column(pos_ref[pl.ds(r, 1), :].astype(jnp.float32))
    have = (lax.broadcasted_iota(jnp.int32, (masked, local_rows), 1) + g * local_rows).astype(jnp.float32)
    load.wait()
    tab_copies = []
    for first in range(0, vocab, BATCH):
        piece = pl.ds(first, min(BATCH, vocab - first))
        tab_copies.append(
            pltpu.make_async_copy(table_hbm.at[piece], table_v.at[piece], tab_sem.at[first // BATCH])
        )
        tab_copies[-1].start()
    one_hot = jnp.where(want == have, 1.0, 0.0).astype(jnp.bfloat16)
    mine = jnp.dot(one_hot, hid_v[...], preferred_element_type=jnp.float32)
    part_out[...] = mine.reshape(group, masked // group, dl).astype(jnp.bfloat16)

    pl.semaphore_wait(barrier, n - 1 + nv - 1)

    for k in range(1, group):
        to = lax.rem(g + k, group)
        remote(part_out.at[to], picked_in.at[g], p1s.at[to], p1r.at[g], voc=r * group + to).start()
    total = part_out[g].astype(jnp.float32)
    for k in range(1, group):
        src = lax.rem(g + k, group)
        remote(part_out.at[src], picked_in.at[src], p1s.at[src], p1r.at[src], voc=r * group + src).wait_recv()
        total += picked_in[src].astype(jnp.float32)
    picked[v] = total.astype(jnp.bfloat16)
    for k in range(1, nr):
        to = lax.rem(r + k, nr)
        remote(picked.at[v], picked.at[v], p2s.at[to], p2r.at[r], voc=to * group + g).start()
    for k in range(nr):
        src = lax.rem(r + k, nr)
        slot = src * group + g
        if k:
            remote(picked.at[slot], picked.at[slot], p2s.at[src], p2r.at[src], voc=slot).wait_recv()
        for j in range(1, group):
            to = lax.rem(g + j, group)
            remote(
                picked.at[slot], picked.at[slot], p3s.at[src, to], p3r.at[src, g], voc=r * group + to
            ).start()
    for k in range(nr):
        src = lax.rem(r + k, nr)
        for j in range(1, group):
            seat = lax.rem(g + j, group)
            slot = src * group + seat
            remote(
                picked.at[slot], picked.at[slot], p3s.at[src, seat], p3r.at[src, seat], voc=r * group + seat
            ).wait_recv()
    gain = gain_ref[...]
    for k in range(nr):
        x = picked[k * group : (k + 1) * group].astype(jnp.float32).reshape(masked, dl)
        square[k * masked : (k + 1) * masked, :] = jnp.broadcast_to(
            jnp.sum(x * x, axis=1, keepdims=True), (masked, LANES)
        )
        scaled[k * masked : (k + 1) * masked, :] = (x * gain).astype(jnp.bfloat16)

    places = (h, n - 1 - h)
    ends = (n - 1, 0)
    steps = (1, -1)
    for side in range(2):
        sq_send[side] = jnp.transpose(square[side * half : (side + 1) * half, :])[:SUB]

        @pl.when(places[side] < n - 1)
        def _(side=side):
            remote(sq_send.at[side], sq_recv.at[h], sqs.at[side], sqr.at[h], hid=ends[side]).start()

    for copy in tab_copies:
        copy.wait()
    run_max[...] = jnp.full(run_max.shape, LOW, jnp.float32)
    run_sum[...] = jnp.zeros_like(run_sum)
    acc[...] = jnp.zeros_like(acc)
    limit = vocab - (tiles - 1) * TILE

    def chain(side, t):
        src = part.at[side, t] if send_buf is None else send_buf.at[side, t]
        to = jnp.clip(h + steps[side], 0, n - 1)
        return remote(src, recv_buf.at[side, t], rss.at[side, t], rsr.at[side, t], hid=to)

    def sum_step(s, carry):
        @pl.when((s < slots) & (lax.rem(s, PAIR) == 0))
        def _():
            piece = pl.ds(pl.multiple_of(s * TILE, TILE), PAIR * TILE)
            both = lax.dot_general(
                scaled[...], table_v[piece, :], (((1,), (1,)), ((), ())),
                preferred_element_type=jnp.float32,
            )
            for k in range(PAIR):
                part[0, s + k] = both[:half, k * TILE : (k + 1) * TILE]
                part[1, s + k] = both[half:, k * TILE : (k + 1) * TILE]

        for side in range(2):
            place = places[side]
            t = s - GAP * place

            @pl.when((t >= 0) & (t < tiles))
            def _(side=side, place=place, t=t):
                @pl.when(place > 0)
                def _():
                    chain(side, t).wait_recv()
                    part[side, t] += recv_buf[side, t].astype(jnp.float32)

                @pl.when(place < n - 1)
                def _():
                    if send_buf is not None:
                        send_buf[side, t] = part[side, t].astype(LINK)
                    chain(side, t).start()

                @pl.when(place == n - 1)
                def _():
                    @pl.when(t == tiles - 1)
                    def _():
                        column = lax.broadcasted_iota(jnp.int32, (half, TILE), 1)
                        part[side, t] = jnp.where(column < limit, part[side, t], LOW)

                    top = run_max[...]
                    for c in range(0, TILE, LANES):
                        top = jnp.maximum(top, part[side, t, :, c : c + LANES])
                    run_max[...] = top

        return carry

    lax.fori_loop(0, tiles + GAP * (n - 1), sum_step, 0)

    def spread(side, t):
        to = jnp.clip(h - steps[side], 0, n - 1)
        return remote(probs.at[side, t], probs.at[side, t], ags.at[side, t], agr.at[side, t], hid=to)

    for side in range(2):

        @pl.when(places[side] == n - 1)
        def _(side=side):
            squares = sq_send[side]
            for k in range(1, n):
                src = lax.rem(h + k, n)
                remote(sq_send.at[side], sq_recv.at[src], sqs.at[side], sqr.at[src], hid=src).wait_recv()
                squares += sq_recv[src]
            inverse = as_column(
                lax.rsqrt(squares[:1] / width + norm_eps) * (logit_scale / math.sqrt(width))
            )
            top = jnp.max(run_max[...], axis=1, keepdims=True) * inverse

            def exp_step(t, carry):
                e = jnp.exp(part[side, t] * inverse - top)
                probs[side, t] = e.astype(jnp.bfloat16)
                spread(side, t).start()
                more = run_sum[...]
                for c in range(0, TILE, LANES):
                    more += e[:, c : c + LANES]
                run_sum[...] = more
                return carry

            lax.fori_loop(0, tiles, exp_step, 0)
            stats[v, 0] = as_row(top)
            stats[v, 1] = as_row(jnp.sum(run_sum[...], axis=1, keepdims=True))
            for k in range(1, nv):
                to = lax.rem(v + k, nv)
                remote(stats.at[v], stats.at[v], sts.at[to], str_.at[v], voc=to).start()
            for k in range(1, nv):
                src = lax.rem(v + k, nv)
                remote(stats.at[src], stats.at[src], sts.at[src], str_.at[src], voc=src).wait_recv()
            high = stats[0, 0]
            for k in range(1, nv):
                high = jnp.maximum(high, stats[k, 0])
            total = jnp.zeros_like(high)
            for k in range(nv):
                total += stats[k, 1] * jnp.exp(stats[k, 0] - high)
            weights[side, 0] = jnp.exp(stats[v, 0] - high) / total
            weights[side, 1] = high - (high + jnp.log(total))
            for k in range(1, n):
                to = lax.rem(h + k, n)
                remote(weights.at[side], weights.at[side], ws.at[to], wr.at[side], hid=to).start()

    for t in range(tiles, slots):
        probs[:, t] = jnp.zeros((2, half, TILE), probs.dtype)
    lag = GAP * jnp.maximum(h, n - 1 - h)

    def mix_step(s, carry):
        for side in range(2):
            place = places[side]
            t = s - GAP * (n - 1 - place)

            @pl.when((t >= 0) & (t < tiles) & (place < n - 1))
            def _(side=side, place=place, t=t):
                spread(side, t).wait_recv()

                @pl.when(place > 0)
                def _():
                    spread(side, t).start()

        m = s - lag

        @pl.when((m >= 0) & (m < slots) & (lax.rem(m, PAIR) == PAIR - 1))
        def _():
            first = m - (PAIR - 1)
            piece = pl.ds(pl.multiple_of(first * TILE, PAIR * TILE), PAIR * TILE)
            both = jnp.concatenate(
                [
                    jnp.concatenate([probs[side, first + k] for k in range(PAIR)], axis=1)
                    for side in range(2)
                ],
                axis=0,
            )
            step = min(dl, 512)
            for c in range(0, dl, step):
                acc[:, c : c + step] += jnp.dot(
                    both, table_v[piece, c : c + step], preferred_element_type=jnp.float32
                )

        return carry

    lax.fori_loop(0, slots + GAP * (n - 1), mix_step, 0)

    for side in range(2):

        @pl.when(places[side] < n - 1)
        def _(side=side):
            remote(
                weights.at[side], weights.at[side], ws.at[ends[side]], wr.at[side], hid=ends[side]
            ).wait_recv()

        scale = as_column(weights[side, 0, :1])
        span = slice(side * half, (side + 1) * half)
        square[span, :] = jnp.broadcast_to(scale, (half, LANES))
    first = v * out_rows
    log_top = as_column(weights[first // half, 1, :1])
    row_of = lax.broadcasted_iota(jnp.int32, (half, out_rows), 0)
    place_of = lax.broadcasted_iota(jnp.int32, (half, out_rows), 1) + lax.rem(first, half)
    stat_ref[...] = jnp.sum(jnp.where(row_of == place_of, log_top, 0.0), axis=0, keepdims=True)

    def block(seat, k):
        start = pl.multiple_of((k * group + seat) * out_rows, out_rows)
        return acc[pl.ds(start, out_rows), :] * square[pl.ds(start, out_rows), :1]

    for k in range(nr):
        there = lax.rem(r + k + 1, nr)
        for j in range(1, group):
            to = lax.rem(g + j, group)
            vx[to, there] = block(to, there).astype(jnp.bfloat16)
            remote(
                vx.at[to, there], v1.at[g, there], e1s.at[to, there], e1r.at[g, there], voc=r * group + to
            ).start()
    total = None
    for k in range(nr):
        there = lax.rem(r + k + 1, nr)
        total = block(g, there)
        for j in range(1, group):
            src = lax.rem(g + j, group)
            remote(
                vx.at[src, there], v1.at[src, there], e1s.at[src, there], e1r.at[src, there],
                voc=r * group + src,
            ).wait_recv()
            total += v1[src, there].astype(jnp.float32)
        if k < nr - 1:
            v2s[there] = total.astype(jnp.bfloat16)
            remote(v2s.at[there], v2.at[r], e2s.at[there], e2r.at[r], voc=there * group + g).start()
        else:
            out_ref[...] = total
    for k in range(1, nr):
        src = lax.rem(r + k, nr)
        remote(v2s.at[src], v2.at[src], e2s.at[src], e2r.at[src], voc=src * group + g).wait_recv()
        out_ref[...] += v2[src].astype(jnp.float32)

    for k in range(1, group):
        to = lax.rem(g + k, group)
        remote(part_out.at[to], picked_in.at[g], p1s.at[to], p1r.at[g], voc=r * group + to).wait_send()
    for k in range(nr):
        src = lax.rem(r + k, nr)
        slot = src * group + g
        if k:
            remote(picked.at[v], picked.at[v], p2s.at[src], p2r.at[r], voc=slot).wait_send()
            remote(v2s.at[src], v2.at[r], e2s.at[src], e2r.at[r], voc=slot).wait_send()
        for j in range(1, group):
            to = lax.rem(g + j, group)
            mate = r * group + to
            remote(picked.at[slot], picked.at[slot], p3s.at[src, to], p3r.at[src, g], voc=mate).wait_send()
            remote(vx.at[to, src], v1.at[g, src], e1s.at[to, src], e1r.at[g, src], voc=mate).wait_send()
    for side in range(2):

        @pl.when(places[side] < n - 1)
        def _(side=side):
            remote(sq_send.at[side], sq_recv.at[h], sqs.at[side], sqr.at[h], hid=ends[side]).wait_send()

        @pl.when(places[side] == n - 1)
        def _(side=side):
            for k in range(1, nv):
                to = lax.rem(v + k, nv)
                remote(stats.at[v], stats.at[v], sts.at[to], str_.at[v], voc=to).wait_send()
            for k in range(1, n):
                to = lax.rem(h + k, n)
                remote(weights.at[side], weights.at[side], ws.at[to], wr.at[side], hid=to).wait_send()

        def drain(t, carry, side=side):
            @pl.when(places[side] < n - 1)
            def _():
                chain(side, t).wait_send()

            @pl.when(places[side] > 0)
            def _():
                spread(side, t).wait_send()

            return carry

        lax.fori_loop(0, tiles, drain, 0)


def local(width, hidden_states, positions, norm_gain, embed_table):
    nr, masked = positions.shape
    rows = nr * masked
    n, nv = lax.axis_size("hid"), lax.axis_size("voc")
    group = nv // nr
    local_rows, dl = hidden_states.shape
    vocab = embed_table.shape[0]
    tiles = pl.cdiv(vocab, TILE)
    slots = pl.cdiv(tiles, PAIR) * PAIR
    half, out_rows = rows // 2, rows // nv
    bf16, f32 = jnp.bfloat16, jnp.float32
    narrow = LINK != jnp.float32
    dma = pltpu.SemaphoreType.DMA
    vmem = pl.BlockSpec(memory_space=pltpu.VMEM)
    hbm = pl.BlockSpec(memory_space=pl.ANY)
    scratch = [
        pltpu.VMEM((local_rows, dl), bf16),
        pltpu.VMEM((slots * TILE, dl), bf16),
        pltpu.VMEM((group, masked // group, dl), bf16),
        pltpu.VMEM((group, masked // group, dl), bf16),
        pltpu.VMEM((nv, masked // group, dl), bf16),
        pltpu.VMEM((rows, dl), bf16),
        pltpu.VMEM((rows, LANES), f32),
        pltpu.VMEM((2, SUB, half), f32),
        pltpu.VMEM((n, SUB, half), f32),
        pltpu.VMEM((2, slots, half, TILE), f32),
        pltpu.VMEM((2, tiles, half, TILE), LINK) if narrow else None,
        pltpu.VMEM((2, tiles, half, TILE), LINK),
        pltpu.VMEM((half, LANES), f32),
        pltpu.VMEM((half, LANES), f32),
        pltpu.VMEM((2, slots, half, TILE), bf16),
        pltpu.VMEM((nv, 2, SUB, half), f32),
        pltpu.VMEM((2, 2, SUB, half), f32),
        pltpu.VMEM((rows, dl), f32),
        pltpu.VMEM((group, nr, out_rows, dl), bf16),
        pltpu.VMEM((group, nr, out_rows, dl), bf16),
        pltpu.VMEM((nr, out_rows, dl), bf16),
        pltpu.VMEM((nr, out_rows, dl), bf16),
        dma, dma((pl.cdiv(vocab, BATCH),)),
        dma((group,)), dma((group,)), dma((nr,)), dma((nr,)), dma((nr, group)), dma((nr, group)),
        dma((2,)), dma((n,)),
        dma((2, tiles)), dma((2, tiles)), dma((2, tiles)), dma((2, tiles)),
        dma((nv,)), dma((nv,)), dma((n,)), dma((2,)),
        dma((group, nr)), dma((group, nr)), dma((nr,)), dma((nr,)),
    ]
    absent = 6 + 10
    body = functools.partial(kernel, (n, nv, nr, width))
    if not narrow:
        scratch = [s for s in scratch if s is not None]

        def body(*refs):
            kernel((n, nv, nr, width), *refs[:absent], None, *refs[absent:])

    expected, stat = pl.pallas_call(
        body,
        out_shape=(
            jax.ShapeDtypeStruct((out_rows, dl), f32),
            jax.ShapeDtypeStruct((1, out_rows), f32),
        ),
        in_specs=[hbm, vmem, vmem, hbm],
        out_specs=(vmem, vmem),
        scratch_shapes=scratch,
        compiler_params=pltpu.CompilerParams(
            collective_id=0, has_side_effects=True, vmem_limit_bytes=60 * 1024 * 1024
        ),
        name="head",
    )(hidden_states, positions, norm_gain.reshape(1, dl), embed_table)
    return expected, stat.reshape(out_rows)


def solution(mesh):
    def whole(hidden_states, positions, norm_gain, embed_table):
        return jax.shard_map(
            functools.partial(local, hidden_states.shape[1]),
            mesh=mesh,
            in_specs=(P("voc", "hid"), P(), P("hid"), P("voc", "hid")),
            out_specs=(P("voc", "hid"), P("voc")),
            check_vma=False,
        )(hidden_states, positions, norm_gain, embed_table)

    return whole
```
